32 devices in a mesh: dp: 8 (over z, y), tensor: 4 (over x, core).
Axes of the slice: x: 2, y: 2, z: 4, core: 2. Of those that a mesh axis runs over, the one named last changes fastest.
Arguments:
- hidden_in: bfloat16 [8192, 2560], P(('dp', 'tensor')), may hold values from -6 to 6
- cotangent: bfloat16 [8192, 2560], P(('dp', 'tensor')), may hold values from -6 to 6
- piece_starts: int32 [8, 2], P('dp'), may hold values from 0 to 768, as said below
- attn_gain: bfloat16 [2560], P('dp'), may hold values from 0.5 to 1.5
- q_a_weight: bfloat16 [2560, 768], P('dp'), may hold values from -0.125 to 0.125
- q_gain: bfloat16 [768], P('dp'), may hold values from 0.5 to 1.5
- q_b_weight: bfloat16 [768, 3840], P('dp', 'tensor'), may hold values from -0.21875 to 0.21875
- kv_a_weight: bfloat16 [2560, 288], P('dp'), may hold values from -0.125 to 0.125
- kv_gain: bfloat16 [256], P('dp'), may hold values from 0.5 to 1.5
- kv_b_weight: bfloat16 [256, 5120], P('dp', 'tensor'), may hold values from -0.375 to 0.375
- o_weight: bfloat16 [2560, 2560], P('tensor', 'dp'), may hold values from -4 to 4
- mlp_gain: bfloat16 [2560], P('dp'), may hold values from 0.5 to 1.5
- gate_weight: bfloat16 [2560, 6400], P('dp', 'tensor'), may hold values from -0.125 to 0.125
- up_weight: bfloat16 [2560, 6400], P('dp', 'tensor'), may hold values from -0.125 to 0.125
- down_weight: bfloat16 [6400, 2560], P('tensor', 'dp'), may hold values from -0.75 to 0.75
Outputs:
- output: bfloat16 [8192, 2560], P(('dp', 'tensor'))
- input_grad: bfloat16 [8192, 2560], P(('dp', 'tensor'))
- attn_gain_grad: float32 [2560], P('dp')
- q_a_grad: float32 [2560, 768], P('dp')
- q_gain_grad: float32 [768], P('dp')
- q_b_grad: float32 [768, 3840], P('dp', 'tensor')
- kv_a_grad: float32 [2560, 288], P('dp')
- kv_gain_grad: float32 [256], P('dp')
- kv_b_grad: float32 [256, 5120], P('dp', 'tensor')
- o_grad: float32 [2560, 2560], P('tensor', 'dp')
- mlp_gain_grad: float32 [2560], P('dp')
- gate_grad: float32 [2560, 6400], P('dp', 'tensor')
- up_grad: float32 [2560, 6400], P('dp', 'tensor')
- down_grad: float32 [6400, 2560], P('tensor', 'dp')
The draws below stay inside these ranges and needn't reach their ends.
Inputs may be any that keep to these rules, and one draw needn't show every extreme that they name: `piece_starts`: piece k of a sequence lies inside positions k * 512 to (k + 1) * 512, so the pieces of a sequence are in order and never intersect.
All inputs are finite; a program needn't handle non-finite values.
Results may differ from the reference program's by a relative error of at most 0.025.
Values may be sent and summed in bfloat16 or wider, within the bound.
No kernel may reach another device: no remote copies, remote signals or barrier semaphores. Data moves between devices by JAX's collectives and lax.ppermute only.
A program may use at most 256 MiB of HBM per device.

```python
import math
import jax
import jax.numpy as jnp
from jax import lax

D = 2560
FF = 6400
HEADS = 40
NOPE = 64
ROPE = 32
VDIM = 64
QRANK = 768
KRANK = 256
LENGTH = 1024
PIECE = 256
PIECES = 2
SEQS = 8
TOKENS = 8192


def draw_piece_starts(key, part):
    region = LENGTH // PIECES
    offsets = jax.random.randint(key, (SEQS, PIECES), 0, region - PIECE + 1)
    row_ids = lax.broadcasted_iota(jnp.int32, (SEQS, PIECES), 0)
    col_ids = lax.broadcasted_iota(jnp.int32, (SEQS, PIECES), 1)
    offsets = jnp.where((row_ids == 0) & (col_ids == 0), 0, offsets)
    offsets = jnp.where((row_ids == 0) & (col_ids == PIECES - 1), region - PIECE, offsets)
    return (col_ids * region + offsets).astype(jnp.int32)


def levels(key, dims, split, low, top_value):
    loudness = 1.0
    for position, shards_of in split:
        steps = jax.random.uniform(jax.random.fold_in(jax.random.fold_in(key, 6), position), (shards_of,), jnp.float32, low / len(split), top_value / len(split))
        loudness = loudness * jnp.repeat(jnp.exp(steps), dims[position] // shards_of).reshape((-1,) + (1,) * (len(dims) - 1 - position))
    return loudness


def centred(key, shape, spread, most, split=(), dtype=jnp.bfloat16):
    drawn = jax.random.normal(key, shape, jnp.float32) * spread
    if len(split) > 0:
        drawn = levels(key, shape, split, -0.22, 0.18) * drawn
    return jnp.clip(drawn, min=-most, max=most).astype(dtype)


def setup_inputs(seed: int = 0) -> dict:
    seeds = jax.random.split(jax.random.key(seed), 16)
    return {
        "hidden_in": centred(seeds[0], (TOKENS, D), 1.0, 6.0, ((0, 32),)),
        "cotangent": centred(seeds[1], (TOKENS, D), 1.0, 6.0, ((0, 32),)),
        "piece_starts": draw_piece_starts(jax.random.fold_in(seeds[15], 71), 0),
        "attn_gain": jnp.clip(1.0 + 0.1 * jax.random.normal(seeds[3], (D,), jnp.float32), 0.5, 1.5).astype(jnp.bfloat16),
        "q_a_weight": centred(seeds[4], (D, QRANK), D ** -0.5, 0.125, ((0, 8),)),
        "q_gain": jnp.clip(1.0 + 0.1 * jax.random.normal(seeds[5], (QRANK,), jnp.float32), 0.5, 1.5).astype(jnp.bfloat16),
        "q_b_weight": centred(seeds[6], (QRANK, HEADS * (NOPE + ROPE)), QRANK ** -0.5, 0.21875, ((0, 8), (1, 4))),
        "kv_a_weight": centred(seeds[7], (D, KRANK + ROPE), D ** -0.5, 0.125, ((0, 8),)),
        "kv_gain": jnp.clip(1.0 + 0.1 * jax.random.normal(seeds[8], (KRANK,), jnp.float32), 0.5, 1.5).astype(jnp.bfloat16),
        "kv_b_weight": centred(seeds[9], (KRANK, HEADS * (NOPE + VDIM)), KRANK ** -0.5, 0.375, ((0, 8), (1, 4))),
        "o_weight": centred(seeds[10], (HEADS * VDIM, D), 2 ** -0.5, 4.0, ((0, 4), (1, 8))),
        "mlp_gain": jnp.clip(1.0 + 0.1 * jax.random.normal(seeds[11], (D,), jnp.float32), 0.5, 1.5).astype(jnp.bfloat16),
        "gate_weight": centred(seeds[12], (D, FF), D ** -0.5, 0.125, ((0, 8), (1, 4))),
        "up_weight": centred(seeds[13], (D, FF), D ** -0.5, 0.125, ((0, 8), (1, 4))),
        "down_weight": centred(seeds[14], (FF, D), 64 ** -0.5, 0.75, ((0, 4), (1, 8))),
    }


norm_eps = 1e-05
res_scale = 1.4 / math.sqrt(62.0)
rope_base = 10000.0
masked_score = -1000000000.0
highest = lax.Precision.HIGHEST

@jax.custom_vjp
def low(v):
    return lax.optimization_barrier(v.astype(jnp.bfloat16)).astype(jnp.float32)

@jax.custom_vjp
def low_back(v):
    return v

def low_keep(v):
    return (low(v), None)

def low_pass(kept, grad):
    return (grad,)

def back_keep(v):
    return (v, None)

def back_low(kept, grad):
    return (low(grad),)
low.defvjp(low_keep, low_pass)
low_back.defvjp(back_keep, back_low)

def matmul(operand_a, operand_b):
    return jnp.dot(operand_a, operand_b, precision=highest, preferred_element_type=jnp.float32)

def rms_scale(values, gain_vec):
    return values * lax.rsqrt(lax.optimization_barrier(jnp.mean(values * values, axis=-1, keepdims=True)) + norm_eps) * gain_vec

def rotary_tables(positions):
    half_dim = ROPE // 2
    frequencies = rope_base ** (-(jnp.arange(half_dim).astype(jnp.float32) * 2.0) / ROPE)
    angles = positions.astype(jnp.float32)[:, None] * frequencies[None, :]
    cos_table = jnp.concatenate([jnp.cos(angles), jnp.cos(angles)], axis=-1)
    sin_table = jnp.concatenate([jnp.sin(angles), jnp.sin(angles)], axis=-1)
    return (cos_table, sin_table)

def rotate(values, cos_table, sin_table):
    half_dim = values.shape[-1] // 2
    turned = jnp.concatenate([-values[..., half_dim:], values[..., :half_dim]], axis=-1)
    return values * cos_table + turned * sin_table

def visible_mask(query_pos, key_pos, starts):
    allowed = key_pos[None, :] <= query_pos[:, None]
    for piece_idx in range(PIECES):
        piece_start = starts[piece_idx]
        query_in = (query_pos >= piece_start) & (query_pos < piece_start + PIECE)
        key_in = (key_pos >= piece_start) & (key_pos < piece_start + PIECE)
        allowed = allowed | query_in[:, None] & key_in[None, :]
    return allowed

def head_attention(query_rows, key_rows, value_rows, starts):
    scores = low_back(matmul(query_rows, key_rows.T) * (1.0 / math.sqrt(NOPE + ROPE)))
    positions = jnp.arange(LENGTH)
    scores = jnp.where(visible_mask(positions, positions, starts), scores, masked_score)
    prob_vals = jax.nn.softmax(scores, axis=-1)
    return matmul(low(prob_vals), value_rows)

def forward(inputs, params, starts):
    attn_gain, q_a, q_gain, q_b, kv_a, kv_gain, kv_b, o_mat, mlp_gain, gate_mat, up_mat, down_mat = params
    cos_table, sin_table = rotary_tables(jnp.arange(LENGTH))
    normed = low(rms_scale(inputs, attn_gain))
    q_latent = low_back(matmul(normed, q_a))
    q_normed = low(rms_scale(q_latent, q_gain))
    queries = low_back(matmul(q_normed, q_b)).reshape(LENGTH, HEADS, NOPE + ROPE)
    kv_latent = low_back(matmul(normed, kv_a))
    kv_normed = low(rms_scale(kv_latent[:, :KRANK], kv_gain))
    key_rot = rotate(kv_latent[:, KRANK:], cos_table, sin_table)
    keyvals = low_back(matmul(kv_normed, kv_b)).reshape(LENGTH, HEADS, NOPE + VDIM)
    query_all = low(jnp.concatenate([queries[..., :NOPE], rotate(queries[..., NOPE:], cos_table[:, None], sin_table[:, None])], axis=-1))
    key_all = low(jnp.concatenate([keyvals[..., :NOPE], jnp.broadcast_to(key_rot[:, None, :], (LENGTH, HEADS, ROPE))], axis=-1))
    value_all = low(keyvals[..., NOPE:])
    checked = jax.checkpoint(head_attention)

    def per_head(head_items):
        return checked(head_items[0], head_items[1], head_items[2], starts)
    heads_out = lax.map(per_head, (jnp.transpose(query_all, (1, 0, 2)), jnp.transpose(key_all, (1, 0, 2)), jnp.transpose(value_all, (1, 0, 2))))
    attn_rows = low_back(low(jnp.transpose(heads_out, (1, 0, 2)).reshape(LENGTH, HEADS * VDIM)))
    branch = low_back(matmul(attn_rows, o_mat))
    hidden = inputs + res_scale * branch
    mlp_in = low(rms_scale(hidden, mlp_gain))
    gate_vals = low_back(matmul(mlp_in, gate_mat))
    up_vals = low_back(matmul(mlp_in, up_mat))
    activations = low(jax.nn.silu(gate_vals) * up_vals)
    mlp_out = low_back(matmul(activations, down_mat))
    return hidden + res_scale * mlp_out

def reference(hidden_in, cotangent, piece_starts, attn_gain, q_a_weight, q_gain, q_b_weight, kv_a_weight, kv_gain, kv_b_weight, o_weight, mlp_gain, gate_weight, up_weight, down_weight):
    params = tuple((weight_arr.astype(jnp.float32) for weight_arr in (attn_gain, q_a_weight, q_gain, q_b_weight, kv_a_weight, kv_gain, kv_b_weight, o_weight, mlp_gain, gate_weight, up_weight, down_weight)))
    seq_inputs = hidden_in.astype(jnp.float32).reshape(SEQS, LENGTH, D)
    seq_grads = cotangent.astype(jnp.float32).reshape(SEQS, LENGTH, D)

    def one_sequence(totals, seq_items):
        seq_in, seq_grad, starts = seq_items

        def apply_layer(layer_in, layer_params):
            return forward(layer_in, layer_params, starts)
        result, pullback = jax.vjp(apply_layer, seq_in, params)
        input_grad, param_grads = pullback(seq_grad)
        totals = jax.tree.map(jnp.add, totals, param_grads)
        return (totals, (result.astype(jnp.bfloat16), input_grad.astype(jnp.bfloat16)))
    zero_grads = tuple((jnp.zeros(weight_arr.shape, jnp.float32) for weight_arr in params))
    totals, (outputs, input_grads) = lax.scan(one_sequence, zero_grads, (seq_inputs, seq_grads, piece_starts))
    return (outputs.reshape(TOKENS, D), input_grads.reshape(TOKENS, D), totals[0], totals[1], totals[2], totals[3], totals[4], totals[5], totals[6], totals[7], totals[8], totals[9], totals[10], totals[11])
```

```python
import functools
import math

import jax
import jax.numpy as jnp
from jax import lax
from jax.experimental import pallas as pl
from jax.experimental.pallas import tpu as pltpu
from jax.sharding import PartitionSpec as P

NOPE = 64
ROPE = 32
HALF = ROPE // 2
QDIM = NOPE + ROPE
VDIM = 64
KVDIM = NOPE + VDIM
KRANK = 256
LENGTH = 1024
PIECE = 256
PIECES = 2
TILE = 256

norm_eps = 1e-05
res_scale = 1.4 / math.sqrt(62.0)
rope_base = 10000.0
score_scale = 1.0 / math.sqrt(QDIM)
log2e = math.log2(math.e)
hidden_bias = -1e30


f32 = jnp.float32
bf16 = jnp.bfloat16


def dot(operand_a, operand_b, dim_a, dim_b):
    return lax.dot_general(
        operand_a, operand_b, (((dim_a,), (dim_b,)), ((), ())), preferred_element_type=f32
    )


def inv_rms_of(values):
    return lax.rsqrt(jnp.mean(values * values, axis=-1, keepdims=True) + norm_eps)


def rms_scale(values, gain_vec):
    return values * inv_rms_of(values) * gain_vec


def rms_back(values, gain_vec, upstream):
    inv_rms = inv_rms_of(values)
    normal = values * inv_rms
    gain_grad = jnp.sum(upstream * normal, axis=0)
    scaled = upstream * gain_vec
    return (
        inv_rms * (scaled - normal * jnp.mean(scaled * normal, axis=-1, keepdims=True)),
        gain_grad,
    )


def rotary_angles(positions):
    frequencies = rope_base ** (-(jnp.arange(HALF).astype(f32) * 2.0) / ROPE)
    return positions.astype(f32)[:, None] * frequencies[None, :]


class Ring:
    def __init__(self, axis):
        self.axis = axis
        self.size = lax.axis_size(axis)
        order = list(range(0, self.size, 2)) + list(range(self.size - 1, 0, -2))
        count = self.size
        self.up = [(order[i], order[(i + 1) % count]) for i in range(count)]
        self.down = [(order[i], order[(i - 1) % count]) for i in range(count)]
        mine = lax.axis_index(axis)
        self.place = jnp.where(mine % 2 == 0, mine // 2, count - 1 - mine // 2)

    def owner(self, offset):
        spot = (self.place + offset + self.size) % self.size
        return jnp.where(spot < self.size // 2, 2 * spot, 2 * self.size - 1 - 2 * spot)

    def gather_chunks(self, chunk, long_up, after=None):
        if after is not None:
            chunk, _ = lax.optimization_barrier((chunk, after))
        half = self.size // 2
        steps_up = half if long_up else half - 1
        found = [(0, chunk)]
        moving_up = moving_down = chunk
        for step in range(1, half + 1):
            if step <= steps_up:
                moving_up = lax.ppermute(moving_up, self.axis, self.up)
                found.append((-step, moving_up))
            if step <= self.size - 1 - steps_up:
                moving_down = lax.ppermute(moving_down, self.axis, self.down)
                found.append((step, moving_down))
        return found

    def assemble(self, found, rows=None):
        rows = found[0][1].shape[0] if rows is None else rows
        cols = found[0][1].shape[1]
        whole = jnp.zeros((rows * self.size, cols), found[0][1].dtype)
        for offset, chunk in found:
            whole = lax.dynamic_update_slice(whole, chunk[:rows], (self.owner(offset) * rows, 0))
        return whole

    def scatter(self, terms, long_up, after=None):
        if after is not None:
            terms, _ = lax.optimization_barrier((terms, after))
        rows = terms.shape[0] // self.size
        half = self.size // 2
        steps_up = half if long_up else half - 1
        steps_down = self.size - 1 - steps_up

        def take(offset):
            return lax.dynamic_slice_in_dim(terms, self.owner(offset) * rows, rows, 0)

        moving_up, moving_down = take(steps_up), take(-steps_down)
        for step in range(1, half + 1):
            if step <= steps_up:
                moving_up = lax.ppermute(moving_up, self.axis, self.up)
                if step < steps_up:
                    moving_up = (
                        moving_up.astype(f32) + take(steps_up - step).astype(f32)
                    ).astype(bf16)
            if step <= steps_down:
                moving_down = lax.ppermute(moving_down, self.axis, self.down)
                if step < steps_down:
                    moving_down = (
                        moving_down.astype(f32) + take(step - steps_down).astype(f32)
                    ).astype(bf16)
        return take(0).astype(f32) + moving_up.astype(f32) + moving_down.astype(f32)


def fill_bias(starts_ref, seq, bias_ref):
    key_row = lax.broadcasted_iota(jnp.int32, (TILE, TILE), 0)
    query_col = lax.broadcasted_iota(jnp.int32, (TILE, TILE), 1)
    per_piece = LENGTH // PIECES // TILE
    for key_tile, query_tile, slot in masked_tiles():
        start = starts_ref[seq, query_tile // per_piece]
        key_pos = key_row + key_tile * TILE
        query_pos = query_col + query_tile * TILE
        inside = (
            (key_pos >= start)
            & (key_pos < start + PIECE)
            & (query_pos >= start)
            & (query_pos < start + PIECE)
        )
        bias_ref[slot] = jnp.where((key_pos <= query_pos) | inside, 0.0, hidden_bias)


def masked_tiles():
    per_piece = LENGTH // PIECES // TILE
    tiles = []
    for query_tile in range(LENGTH // TILE):
        for key_tile in range(query_tile, LENGTH // TILE):
            if key_tile // per_piece == query_tile // per_piece:
                tiles.append((key_tile, query_tile, len(tiles)))
    return tiles


def tile_slots():
    slots = {(key_tile, query_tile): slot for key_tile, query_tile, slot in masked_tiles()}
    per_piece = LENGTH // PIECES // TILE
    plan = []
    for query_tile in range(LENGTH // TILE):
        last = (query_tile // per_piece + 1) * per_piece
        plan.append([(key_tile, slots.get((key_tile, query_tile))) for key_tile in range(last)])
    return plan


def attend_forward(
    starts_ref, query_ref, keyval_ref, rot_ref, cos_ref, sin_ref, out_ref, turned_ref, lse_ref,
    bias_ref
):
    seq = pl.program_id(0)

    @pl.when(pl.program_id(1) == 0)
    def _():
        fill_bias(starts_ref, seq, bias_ref)

    cos_t, sin_t = cos_ref[...], sin_ref[...]
    first, second = query_ref[NOPE : NOPE + HALF, :], query_ref[NOPE + HALF :, :]
    turned_ref[:NOPE, :] = query_ref[:NOPE, :].astype(bf16)
    turned_ref[NOPE : NOPE + HALF, :] = (first * cos_t - second * sin_t).astype(bf16)
    turned_ref[NOPE + HALF :, :] = (second * cos_t + first * sin_t).astype(bf16)
    keys = jnp.concatenate([keyval_ref[:NOPE, :], rot_ref[...]], axis=0).T
    for query_tile, key_tiles in enumerate(tile_slots()):
        cols = slice(query_tile * TILE, (query_tile + 1) * TILE)
        query = turned_ref[:, cols]
        logits = []
        top = None
        for key_tile, slot in key_tiles:
            part = dot(keys[key_tile * TILE : (key_tile + 1) * TILE, :], query, 1, 0) * (
                score_scale * log2e
            )
            if slot is not None:
                part = part + bias_ref[slot]
            logits.append(part)
            part_top = jnp.max(part, axis=0, keepdims=True)
            top = part_top if top is None else jnp.maximum(top, part_top)
        total = None
        out = None
        for (key_tile, slot), part in zip(key_tiles, logits):
            prob = jnp.exp2(part - top)
            part_total = jnp.sum(prob, axis=0, keepdims=True)
            value = keyval_ref[NOPE:, key_tile * TILE : (key_tile + 1) * TILE]
            part_out = dot(value, prob.astype(bf16), 1, 0)
            total = part_total if total is None else total + part_total
            out = part_out if out is None else out + part_out
        out_ref[:, cols] = (out / total).astype(bf16)
        lse_ref[0, :, cols] = top + jnp.log2(total)


def attend_backward(
    starts_ref, turned_ref, keyval_ref, rot_ref, cos_ref, sin_ref, out_ref, grad_ref, lse_ref,
    query_grad_ref, keyval_grad_ref, rot_grad_ref, bias_ref, key_acc_ref, value_acc_ref
):
    seq = pl.program_id(0)
    head = pl.program_id(1)

    @pl.when(head == 0)
    def _():
        fill_bias(starts_ref, seq, bias_ref)

    keys_t = jnp.concatenate([keyval_ref[:NOPE, :], rot_ref[...]], axis=0)
    keys = keys_t.T
    values = keyval_ref[NOPE:, :].T
    queries = turned_ref[...].T
    grads = grad_ref[...].T
    delta_all = jnp.sum(grad_ref[...].astype(f32) * out_ref[...].astype(f32), axis=0, keepdims=True)
    cos_t, sin_t = cos_ref[...], sin_ref[...]
    touched = set()
    for query_tile, key_tiles in enumerate(tile_slots()):
        cols = slice(query_tile * TILE, (query_tile + 1) * TILE)
        query_t = turned_ref[:, cols]
        grad_t = grad_ref[:, cols]
        query = queries[cols, :]
        grad = grads[cols, :]
        lse = lse_ref[0, :, cols]
        delta = delta_all[:, cols]
        query_grad = None
        for key_tile, slot in key_tiles:
            rows = slice(key_tile * TILE, (key_tile + 1) * TILE)
            part = dot(keys[rows, :], query_t, 1, 0) * (score_scale * log2e)
            if slot is not None:
                part = part + bias_ref[slot]
            prob = jnp.exp2(part - lse)
            prob_grad = dot(values[rows, :], grad_t, 1, 0)
            score_grad = (prob * (prob_grad - delta)).astype(bf16)
            key_part = dot(score_grad, query, 1, 0)
            value_part = dot(prob.astype(bf16), grad, 1, 0)
            if key_tile in touched:
                key_acc_ref[rows, :] += key_part
                value_acc_ref[rows, :] += value_part
            else:
                key_acc_ref[rows, :] = key_part
                value_acc_ref[rows, :] = value_part
                touched.add(key_tile)
            query_part = dot(keys_t[:, rows], score_grad, 1, 0)
            query_grad = query_part if query_grad is None else query_grad + query_part
        query_grad = query_grad * score_scale
        first, second = query_grad[NOPE : NOPE + HALF, :], query_grad[NOPE + HALF :, :]
        cos_b, sin_b = cos_t[:, cols], sin_t[:, cols]
        query_grad_ref[:NOPE, cols] = query_grad[:NOPE, :].astype(bf16)
        query_grad_ref[NOPE : NOPE + HALF, cols] = (first * cos_b + second * sin_b).astype(bf16)
        query_grad_ref[NOPE + HALF :, cols] = (second * cos_b - first * sin_b).astype(bf16)
    key_grad = key_acc_ref[...].T * score_scale
    keyval_grad_ref[:NOPE, :] = key_grad[:NOPE, :].astype(bf16)
    keyval_grad_ref[NOPE:, :] = value_acc_ref[...].T.astype(bf16)

    @pl.when(head == 0)
    def _():
        rot_grad_ref[...] = key_grad[NOPE:, :]

    @pl.when(head > 0)
    def _():
        rot_grad_ref[...] += key_grad[NOPE:, :]


def head_block(rows):
    return pl.BlockSpec((rows, LENGTH), lambda s, h, starts: (h, s))


def seq_block(rows):
    return pl.BlockSpec((rows, LENGTH), lambda s, h, starts: (0, s))


def shared_block(rows):
    return pl.BlockSpec((rows, LENGTH), lambda s, h, starts: (0, 0))


lse_block = pl.BlockSpec((1, 1, LENGTH), lambda s, h, starts: (h, 0, s))


def run_forward(starts, query_t, keyval_t, rot_t, cos_t, sin_t):
    tokens = query_t.shape[1]
    heads = query_t.shape[0] // QDIM
    seqs = tokens // LENGTH
    tiles = len(masked_tiles())
    pairs = seqs * heads * LENGTH * LENGTH * 3 // 4
    return pl.pallas_call(
        attend_forward,
        name="attend_forward",
        grid_spec=pltpu.PrefetchScalarGridSpec(
            num_scalar_prefetch=1,
            grid=(seqs, heads),
            in_specs=[
                head_block(QDIM),
                head_block(KVDIM),
                seq_block(ROPE),
                shared_block(HALF),
                shared_block(HALF),
            ],
            out_specs=[head_block(VDIM), head_block(QDIM), lse_block],
            scratch_shapes=[pltpu.VMEM((tiles, TILE, TILE), f32)],
        ),
        out_shape=[
            jax.ShapeDtypeStruct((heads * VDIM, tokens), bf16),
            jax.ShapeDtypeStruct((heads * QDIM, tokens), bf16),
            jax.ShapeDtypeStruct((heads, 1, tokens), f32),
        ],
        cost_estimate=pl.CostEstimate(
            flops=pairs * 2 * 512, transcendentals=pairs, bytes_accessed=12 << 20
        ),
    )(starts, query_t, keyval_t, rot_t, cos_t, sin_t)


def run_backward(starts, turned_t, keyval_t, rot_t, cos_t, sin_t, out_t, grad_t, lse):
    tokens = turned_t.shape[1]
    heads = turned_t.shape[0] // QDIM
    seqs = tokens // LENGTH
    tiles = len(masked_tiles())
    pairs = seqs * heads * LENGTH * LENGTH * 3 // 4
    return pl.pallas_call(
        attend_backward,
        name="attend_backward",
        grid_spec=pltpu.PrefetchScalarGridSpec(
            num_scalar_prefetch=1,
            grid=(seqs, heads),
            in_specs=[
                head_block(QDIM),
                head_block(KVDIM),
                seq_block(ROPE),
                shared_block(HALF),
                shared_block(HALF),
                head_block(VDIM),
                head_block(VDIM),
                lse_block,
            ],
            out_specs=[head_block(QDIM), head_block(KVDIM), seq_block(ROPE)],
            scratch_shapes=[
                pltpu.VMEM((tiles, TILE, TILE), f32),
                pltpu.VMEM((LENGTH, QDIM), f32),
                pltpu.VMEM((LENGTH, VDIM), f32),
            ],
        ),
        out_shape=[
            jax.ShapeDtypeStruct((heads * QDIM, tokens), bf16),
            jax.ShapeDtypeStruct((heads * KVDIM, tokens), bf16),
            jax.ShapeDtypeStruct((ROPE, tokens), f32),
        ],
        cost_estimate=pl.CostEstimate(
            flops=pairs * 2 * 1280, transcendentals=pairs, bytes_accessed=16 << 20
        ),
    )(starts, turned_t, keyval_t, rot_t, cos_t, sin_t, out_t, grad_t, lse)


def shards(
    hidden_in,
    cotangent,
    piece_starts,
    attn_gain,
    q_a_weight,
    q_gain,
    q_b_weight,
    kv_a_weight,
    kv_gain,
    kv_b_weight,
    o_weight,
    mlp_gain,
    gate_weight,
    up_weight,
    down_weight,
):
    ring = Ring("dp")
    tensor_size = lax.axis_size("tensor")
    tensor_place = lax.axis_index("tensor")
    own_rows = hidden_in.shape[0]
    group_rows = own_rows * tensor_size
    depth = q_a_weight.shape[0]
    q_rank = q_a_weight.shape[1]
    latent = q_rank + kv_a_weight.shape[1]
    width = hidden_in.shape[1]

    gains = jnp.concatenate([attn_gain, mlp_gain, q_gain, kv_gain])
    gain_row = jnp.pad(gains, (0, latent - gains.shape[0]))[None, :]
    down_chunks = jnp.concatenate(
        [
            jnp.concatenate([q_a_weight, kv_a_weight], axis=1),
            jnp.pad(gain_row, ((0, 7), (0, 0))),
        ],
        axis=0,
    )
    a_found = ring.gather_chunks(down_chunks, True)
    q_b_found = ring.gather_chunks(q_b_weight, False)
    kv_b_found = ring.gather_chunks(kv_b_weight, True)
    o_found = ring.gather_chunks(o_weight.T, False, a_found[3][1])
    gate_found = ring.gather_chunks(gate_weight, True, q_b_found[-1][1])
    up_found = ring.gather_chunks(up_weight, False, gate_found[3][1])
    down_found = ring.gather_chunks(down_weight.T, True, up_found[3][1])
    a_all = ring.assemble(a_found, depth)
    gain_rows = ring.assemble([(offset, chunk[depth : depth + 1]) for offset, chunk in a_found])
    q_b_all = ring.assemble(q_b_found)
    kv_b_all = ring.assemble(kv_b_found)
    o_all = ring.assemble(o_found)
    gate_all = ring.assemble(gate_found)
    up_all = ring.assemble(up_found)
    down_all = ring.assemble(down_found)
    cuts = [0]
    for part in (attn_gain, mlp_gain, q_gain, kv_gain):
        cuts.append(cuts[-1] + part.shape[0])
    attn_gain_f, mlp_gain_f, q_gain_f, kv_gain_f = (
        gain_rows[:, cuts[i] : cuts[i + 1]].reshape(-1).astype(f32) for i in range(4)
    )

    own_angles = rotary_angles((tensor_place * own_rows + jnp.arange(own_rows)) % LENGTH)
    own_cos, own_sin = jnp.cos(own_angles), jnp.sin(own_angles)
    seq_angles = rotary_angles(jnp.arange(LENGTH)).T
    cos_t, sin_t = jnp.cos(seq_angles), jnp.sin(seq_angles)
    inputs = hidden_in.astype(f32)
    normed = rms_scale(inputs, attn_gain_f).astype(bf16)
    latents = dot(normed, a_all, 1, 0)
    q_latent = latents[:, :q_rank]
    kv_latent = latents[:, q_rank : q_rank + KRANK]
    first = latents[:, q_rank + KRANK : q_rank + KRANK + HALF]
    second = latents[:, q_rank + KRANK + HALF :]
    own_lat = jnp.concatenate(
        [
            rms_scale(q_latent, q_gain_f),
            rms_scale(kv_latent, kv_gain_f),
            first * own_cos - second * own_sin,
            second * own_cos + first * own_sin,
        ],
        axis=1,
    ).astype(bf16)
    lat_group = lax.all_gather(own_lat, "tensor", axis=0, tiled=True)
    q_normed = lat_group[:, :q_rank]
    kv_normed = lat_group[:, q_rank : q_rank + KRANK]
    rot_t = lat_group[:, q_rank + KRANK :].T
    query_t = dot(q_b_all, q_normed, 0, 1)
    keyval_t = dot(kv_b_all, kv_normed, 0, 1).astype(bf16)
    out_t, turned_t, lse = run_forward(piece_starts, query_t, keyval_t, rot_t, cos_t, sin_t)
    branch = lax.psum_scatter(
        dot(out_t, o_all, 0, 1).astype(bf16), "tensor", scatter_dimension=0, tiled=True
    ).astype(f32)
    hidden = inputs + res_scale * branch
    mlp_in = rms_scale(hidden, mlp_gain_f).astype(bf16)
    mlp_group = lax.all_gather(mlp_in, "tensor", axis=0, tiled=True)
    out_grad = cotangent.astype(f32)
    mlp_grad = (res_scale * out_grad).astype(bf16)
    mlp_grad_group = lax.all_gather(mlp_grad, "tensor", axis=0, tiled=True)
    normed_group = lax.all_gather(normed, "tensor", axis=0, tiled=True)
    gate_vals = dot(mlp_group, gate_all, 1, 0)
    up_vals = dot(mlp_group, up_all, 1, 0)
    activations = (jax.nn.silu(gate_vals) * up_vals).astype(bf16)
    down_grad = dot(mlp_grad_group, activations, 0, 0).astype(bf16)
    down_out = ring.scatter(down_grad, True)
    mlp_out = lax.psum_scatter(
        dot(activations, down_all, 1, 1).astype(bf16), "tensor", scatter_dimension=0, tiled=True
    ).astype(f32)
    result = (hidden + res_scale * mlp_out).astype(bf16)

    act_grad = dot(mlp_grad_group, down_all, 1, 0)
    sigmoid_g = jax.nn.sigmoid(gate_vals)
    gate_rows = (act_grad * up_vals * sigmoid_g * (1.0 + gate_vals * (1.0 - sigmoid_g))).astype(
        bf16
    )
    up_rows = (act_grad * gate_vals * sigmoid_g).astype(bf16)
    mlp_in_grad = lax.psum_scatter(
        (dot(gate_rows, gate_all, 1, 1) + dot(up_rows, up_all, 1, 1)).astype(bf16),
        "tensor",
        scatter_dimension=0,
        tiled=True,
    ).astype(f32)
    gate_grad = dot(mlp_group, gate_rows, 0, 0).astype(bf16)
    up_grad = dot(mlp_group, up_rows, 0, 0).astype(bf16)
    gate_out = ring.scatter(gate_grad, False)
    up_out = ring.scatter(up_grad, True)
    norm_grad, mlp_gain_grad = rms_back(hidden, mlp_gain_f, mlp_in_grad)
    hidden_grad = out_grad + norm_grad
    attn_grad = (res_scale * hidden_grad).astype(bf16)
    attn_grad_group = lax.all_gather(attn_grad, "tensor", axis=0, tiled=True)

    rows_grad_t = dot(o_all, attn_grad_group, 0, 1).astype(bf16)
    o_grad = dot(attn_grad_group, out_t, 0, 1).astype(bf16)
    o_out = ring.scatter(o_grad, False)
    q_raw_t, kv_raw_t, rot_grad_t = run_backward(
        piece_starts, turned_t, keyval_t, rot_t, cos_t, sin_t, out_t, rows_grad_t, lse
    )
    lat_terms = jnp.concatenate(
        [dot(q_raw_t, q_b_all, 0, 1), dot(kv_raw_t, kv_b_all, 0, 1), rot_grad_t.T], axis=1
    ).astype(bf16)
    lat_sum = lax.psum_scatter(lat_terms, "tensor", scatter_dimension=0, tiled=True).astype(f32)
    q_b_out = ring.scatter(dot(q_normed, q_raw_t, 0, 1).astype(bf16), True)
    kv_b_out = ring.scatter(dot(kv_normed, kv_raw_t, 0, 1).astype(bf16), False)
    q_lat_grad, q_gain_grad = rms_back(q_latent, q_gain_f, lat_sum[:, :q_rank])
    kv_lat_grad, kv_gain_grad = rms_back(
        kv_latent, kv_gain_f, lat_sum[:, q_rank : q_rank + KRANK]
    )
    first = lat_sum[:, q_rank + KRANK : q_rank + KRANK + HALF]
    second = lat_sum[:, q_rank + KRANK + HALF :]
    lat_low = jnp.concatenate(
        [
            q_lat_grad,
            kv_lat_grad,
            first * own_cos + second * own_sin,
            second * own_cos - first * own_sin,
        ],
        axis=1,
    ).astype(bf16)
    lat_low_group = lax.all_gather(lat_low, "tensor", axis=0, tiled=True)
    normed_grad = dot(lat_low, a_all, 1, 1)
    input_norm_grad, attn_gain_grad = rms_back(inputs, attn_gain_f, normed_grad)
    input_grad = (hidden_grad + input_norm_grad).astype(bf16)

    share = latent // tensor_size
    lat_share = lat_low_group[:, :share]
    for place in range(1, tensor_size):
        lat_share = jnp.where(
            tensor_place == place, lat_low_group[:, place * share : (place + 1) * share], lat_share
        )
    a_grad = dot(normed_group, lat_share, 0, 0).astype(bf16)
    gain_terms = jnp.concatenate(
        [
            part.astype(bf16).reshape(ring.size, -1)
            for part in (attn_gain_grad, mlp_gain_grad, q_gain_grad, kv_gain_grad)
        ],
        axis=1,
    )
    gain_lines = -(-gain_terms.shape[1] // share)
    gain_pad = -(-gain_lines // 8) * 8
    gain_terms = jnp.pad(
        gain_terms, ((0, 0), (0, gain_pad * share - gain_terms.shape[1]))
    ).reshape(ring.size, gain_pad, share)
    a_terms = jnp.concatenate(
        [a_grad.reshape(ring.size, depth, share), gain_terms], axis=1
    ).reshape(-1, share)
    a_share = ring.scatter(a_terms, False).astype(bf16)
    a_parts = lax.all_gather(a_share, "tensor", axis=0).astype(f32)
    a_out = jnp.transpose(a_parts[:, :depth], (1, 0, 2)).reshape(depth, latent)
    gain_out = jnp.sum(a_parts[:, depth:], axis=0).reshape(-1)
    attn_gain_out, mlp_gain_out, q_gain_out, kv_gain_out = (
        gain_out[cuts[i] : cuts[i + 1]] for i in range(4)
    )
    return (
        result,
        input_grad,
        attn_gain_out,
        a_out[:, :q_rank],
        q_gain_out,
        q_b_out,
        a_out[:, q_rank:],
        kv_gain_out,
        kv_b_out,
        o_out.T,
        mlp_gain_out,
        gate_out,
        up_out,
        down_out.T,
    )


def solution(mesh):
    placed = (
        P(("dp", "tensor"), None),
        P(("dp", "tensor"), None),
        P("dp", None),
        P("dp"),
        P("dp", None),
        P("dp"),
        P("dp", "tensor"),
        P("dp", None),
        P("dp"),
        P("dp", "tensor"),
        P("tensor", "dp"),
        P("dp"),
        P("dp", "tensor"),
        P("dp", "tensor"),
        P("tensor", "dp"),
    )
    return jax.shard_map(
        shards,
        mesh=mesh,
        in_specs=placed,
        out_specs=(
            P(("dp", "tensor"), None),
            P(("dp", "tensor"), None),
            P("dp"),
            P("dp", None),
            P("dp"),
            P("dp", "tensor"),
            P("dp", None),
            P("dp"),
            P("dp", "tensor"),
            P("tensor", "dp"),
            P("dp"),
            P("dp", "tensor"),
            P("dp", "tensor"),
            P("tensor", "dp"),
        ),
        check_vma=False,
    )
```
